32 devices in a mesh: replica: 2 (over y), tensor: 16 (over z, x, core).
Axes of the slice: x: 2, y: 2, z: 4, core: 2. Of those that a mesh axis runs over, the one named last changes fastest.
Arguments:
- tokens: bfloat16 [256, 2560], P('replica', 'tensor'), may hold values from -6 to 6
- next_tokens: bfloat16 [128, 2560], P('replica', 'tensor'), may hold values from -6 to 6
- cotangent: bfloat16 [256, 2560], P('replica', 'tensor'), may hold values from -0.5 to 0.5
- gate_weight: bfloat16 [2560, 14336], P(None, 'tensor'), may hold values from -0.125 to 0.125
- up_weight: bfloat16 [2560, 14336], P(None, 'tensor'), may hold values from -0.125 to 0.125
- down_weight: bfloat16 [14336, 2560], P('tensor'), may hold values from -0.046875 to 0.046875
- momentum: bfloat16 [2, 14336, 2560], P('replica', 'tensor'), may hold values from -6 to 6
- indices: int32 [2, 224, 40, 32], P(None, 'tensor'), may hold values from 0 to 4095, as said below
Outputs:
- output: bfloat16 [128, 2560], P(('replica', 'tensor'))
- new_momentum: bfloat16 [2, 14336, 2560], P('replica', 'tensor')
The draws below stay inside these ranges and needn't reach their ends.
Inputs may be any that keep to these rules, and one draw needn't show every extreme that they name: Within one replica and tile the 32 indices are distinct; the n-th lies in the range from n * 64 * 2 to (n + 1) * 64 * 2 - 1.
All inputs are finite; a program needn't handle non-finite values.
Results may differ from the reference program's by a relative error of at most 0.017.
Values may be sent and summed in bfloat16 or wider, within the bound.
A program may use at most 128 MiB of HBM per device.

```python
import jax
import jax.numpy as jnp
from jax import lax

D = 2560
FF = 14336
TILE = 64
KEEP = 32
TOK = 128
REPLICAS = 2
TOKENS = 256
NEXTS = 128


def draw_indices(key, part):
    stride = TILE * TILE // KEEP
    shape = (REPLICAS, FF // TILE, D // TILE, KEEP)
    offsets = jax.random.randint(key, shape, 0, stride, dtype=jnp.int32)
    base = jnp.arange(KEEP, dtype=jnp.int32) * stride
    return (offsets + base).astype(jnp.int32)


def levels(rng, extent, split, smallest, largest):
    def one(position, blocks):
        steps = jax.random.uniform(jax.random.fold_in(jax.random.fold_in(rng, 6), position), (blocks,), jnp.float32, smallest / len(split), largest / len(split))
        return jnp.repeat(jnp.exp(steps), extent[position] // blocks).reshape((-1,) + (1,) * (len(extent) - position - 1))

    factor_of = one(*split[0])
    for cut in split[1:]:
        factor_of = factor_of * one(*cut)
    return factor_of


def scatter_about(rng, shape, width, bound, cuts=(), kind=jnp.bfloat16):
    entries = width * jax.random.normal(rng, shape, jnp.float32)
    if cuts:
        entries = entries * levels(rng, shape, cuts, -0.22, 0.18)
    return jnp.clip(entries, -bound, bound).astype(kind)


def setup_inputs(seed: int = 0) -> dict:
    key_list = jax.random.split(jax.random.key(seed), 9)
    return {
        "tokens": scatter_about(key_list[0], (TOKENS, D), 1.0, 6.0, ((0, 2), (1, 16))),
        "next_tokens": scatter_about(key_list[1], (NEXTS, D), 1.0, 6.0, ((0, 2), (1, 16))),
        "cotangent": scatter_about(key_list[2], (TOKENS, D), 0.07, 0.5, ((0, 2), (1, 16))),
        "gate_weight": scatter_about(key_list[3], (D, FF), D ** -0.5, 0.125, ((1, 16),)),
        "up_weight": scatter_about(key_list[4], (D, FF), D ** -0.5, 0.125, ((1, 16),)),
        "down_weight": scatter_about(key_list[5], (FF, D), FF ** -0.5, 0.046875, ((0, 16),)),
        "momentum": scatter_about(key_list[6], (REPLICAS, FF, D), 1.0, 6.0, ((0, 2), (1, 16))),
        "indices": draw_indices(jax.random.fold_in(key_list[8], 71), 0),
    }


BETA_DECAY = 0.9
STEP_RATE = 0.1

def cosine_table():
    freq = jnp.arange(TILE, dtype=jnp.float32)[:, None]
    place = jnp.arange(TILE, dtype=jnp.float32)[None, :]
    table = jnp.cos(jnp.pi * (2.0 * place + 1.0) * freq / (2.0 * TILE))
    factor = jnp.where(freq == 0.0, jnp.sqrt(1.0 / TILE), jnp.sqrt(2.0 / TILE))
    return (table * factor).astype(jnp.float32)

def forward_tiles(field, table):
    height, breadth = field.shape
    blocks = field.reshape(height // TILE, TILE, breadth // TILE, TILE)
    spectrum = jnp.einsum('ak,xkyl,bl->xyab', table, blocks, table, precision=lax.Precision.HIGHEST)
    return spectrum.reshape(height // TILE, breadth // TILE, TILE * TILE)

def inverse_tiles(spectrum, table):
    tile_rows, tile_cols, _ = spectrum.shape
    blocks = spectrum.reshape(tile_rows, tile_cols, TILE, TILE)
    field = jnp.einsum('ak,xyab,bl->xkyl', table, blocks, table, precision=lax.Precision.HIGHEST)
    return field.reshape(tile_rows * TILE, tile_cols * TILE)

def place_values(values, where):
    tile_rows, tile_cols, _ = where.shape
    dense = jnp.zeros((tile_rows, tile_cols, TILE * TILE), jnp.float32)
    row_ids = jnp.arange(tile_rows, dtype=jnp.int32)[:, None, None]
    col_ids = jnp.arange(tile_cols, dtype=jnp.int32)[None, :, None]
    return dense.at[row_ids, col_ids, where].add(values)

def swiglu(inputs, gate_weight, up_weight):
    gate = jnp.dot(inputs, gate_weight, preferred_element_type=jnp.float32)
    upper = jnp.dot(inputs, up_weight, preferred_element_type=jnp.float32)
    return (jax.nn.silu(gate) * upper).astype(jnp.bfloat16)

def reference(tokens, next_tokens, cotangent, gate_weight, up_weight, down_weight, momentum, indices):
    table = cosine_table()

    def one_replica(replica):
        start = replica * TOK
        inputs = lax.dynamic_slice_in_dim(tokens, start, TOK, 0)
        grads_out = lax.dynamic_slice_in_dim(cotangent, start, TOK, 0)
        hidden = swiglu(inputs, gate_weight, up_weight)
        grad = jnp.dot(hidden.T, grads_out, preferred_element_type=jnp.float32)
        moment = BETA_DECAY * momentum[replica].astype(jnp.float32) + grad
        spectrum = forward_tiles(moment, table)
        where = indices[replica]
        sent = jnp.take_along_axis(spectrum, where, axis=2).astype(jnp.bfloat16)
        own = place_values(sent.astype(jnp.float32), where)
        kept = (moment - inverse_tiles(own, table)).astype(jnp.bfloat16)
        return (sent, kept)
    sent_all, new_momentum = lax.map(one_replica, jnp.arange(REPLICAS, dtype=jnp.int32))
    where_all = jnp.moveaxis(indices, 0, 2).reshape(FF // TILE, D // TILE, REPLICAS * KEEP)
    values_all = jnp.moveaxis(sent_all.astype(jnp.float32), 0, 2).reshape(FF // TILE, D // TILE, REPLICAS * KEEP)
    total = place_values(values_all, where_all)
    update = inverse_tiles(total, table) / REPLICAS
    new_down = (down_weight.astype(jnp.float32) - STEP_RATE * update).astype(jnp.bfloat16)
    next_hidden = swiglu(next_tokens, gate_weight, up_weight)
    output = jnp.dot(next_hidden, new_down, preferred_element_type=jnp.float32).astype(jnp.bfloat16)
    return (output, new_momentum)
```

```python
import functools

import jax
import jax.numpy as jnp
import numpy as np
from jax import lax
from jax.experimental import pallas as pl
from jax.experimental.pallas import tpu as pltpu
from jax.sharding import PartitionSpec as P

TILE = 64
BETA_DECAY = 0.9
STEP_RATE = 0.1
MESH = pl.DeviceIdType.MESH
VMEM = pl.BlockSpec(memory_space=pltpu.VMEM)


def cosine_table():
    freq = np.arange(TILE)[:, None]
    place = np.arange(TILE)[None, :]
    table = np.cos(np.pi * (2.0 * place + 1.0) * freq / (2.0 * TILE))
    return table * np.where(freq == 0, np.sqrt(1.0 / TILE), np.sqrt(2.0 / TILE))


def split_bf16(table):
    high = jnp.asarray(table, jnp.float32).astype(jnp.bfloat16)
    rest = jnp.asarray(table, jnp.float32) - high.astype(jnp.float32)
    return high, rest.astype(jnp.bfloat16)


def tables(strip, chunk):
    table = cosine_table()
    across = np.kron(np.eye(chunk // TILE), table)
    down = np.concatenate(
        [np.kron(np.eye(strip), table[0::2]), np.kron(np.eye(strip), table[1::2])], axis=0
    )
    row_high, row_low = split_bf16(down)
    col_high, col_low = split_bf16(across.T)
    row = jnp.concatenate([row_high, row_low], axis=1)
    inverse_row = jnp.asarray(down.T, jnp.float32).astype(jnp.bfloat16)
    inverse_col = jnp.asarray(across, jnp.float32).astype(jnp.bfloat16)
    return row, col_high, col_low, inverse_row, inverse_col


def flip(index, bits):
    bit = 1
    while bit <= bits:
        if bits & bit:
            index = index + bit - 2 * bit * ((index // bit) % 2)
        bit *= 2
    return index


def greet(axis, others):
    barrier = pltpu.get_barrier_semaphore()
    for other in others:
        pl.semaphore_signal(barrier, inc=1, device_id={axis: other}, device_id_type=MESH)
    pl.semaphore_wait(barrier, len(others))


def gather_kernel(size, block, out, send, recv, local):
    me = lax.axis_index("tensor")
    depth = size // 4
    z, x, core = me // 4, (me // 2) % 2, me % 2

    def slot(zz, xx, cc):
        return (zz * 2 + xx) * 2 + cc

    others = [flip(z, k) for k in range(1, depth)]
    side, twin = slot(z, 1 - x, core), slot(z, x, 1 - core)
    greet("tensor", [slot(zz, x, core) for zz in others] + [side, twin])
    own = pltpu.make_async_copy(block, out.at[me], local)
    own.start()
    copies = []

    def push(source, which, target):
        copy = pltpu.make_async_remote_copy(
            src_ref=source,
            dst_ref=out.at[which],
            send_sem=send.at[len(copies)],
            recv_sem=recv.at[which],
            device_id={"tensor": target},
            device_id_type=MESH,
        )
        copy.start()
        copies.append(copy)

    def arrive(which):
        pltpu.make_async_remote_copy(
            src_ref=block,
            dst_ref=out.at[which],
            send_sem=send.at[0],
            recv_sem=recv.at[which],
            device_id={"tensor": twin},
            device_id_type=MESH,
        ).wait_recv()

    push(block, me, side)
    for zz in others:
        push(block, me, slot(zz, x, core))
    push(block, me, twin)
    last = z
    for zz in others:
        which = slot(zz, x, core)
        arrive(which)
        push(out.at[which], which, side)
        push(out.at[which], which, twin)
        which = slot(last, 1 - x, core)
        arrive(which)
        push(out.at[which], which, twin)
        last = zz
    which = slot(last, 1 - x, core)
    arrive(which)
    push(out.at[which], which, twin)
    for zz in [z] + others:
        arrive(slot(zz, x, 1 - core))
        arrive(slot(zz, 1 - x, 1 - core))
    own.wait()
    for copy in copies:
        copy.wait_send()


def gather_blocks(block, size):
    return pl.pallas_call(
        functools.partial(gather_kernel, size),
        out_shape=jax.ShapeDtypeStruct((size,) + block.shape, block.dtype),
        in_specs=[VMEM],
        out_specs=VMEM,
        scratch_shapes=[
            pltpu.SemaphoreType.DMA((size,)),
            pltpu.SemaphoreType.DMA((size,)),
            pltpu.SemaphoreType.DMA,
        ],
        compiler_params=pltpu.CompilerParams(collective_id=0, has_side_effects=True),
        name="gather_blocks",
    )(block)


def exchange_kernel(replicas, values, out, send, recv):
    me = lax.axis_index("replica")
    greet("replica", [(me + k) % replicas for k in range(1, replicas)])
    copies = []
    for k in range(1, replicas):
        copy = pltpu.make_async_remote_copy(
            src_ref=values,
            dst_ref=out.at[k - 1],
            send_sem=send.at[k - 1],
            recv_sem=recv.at[k - 1],
            device_id={"replica": (me - k + replicas) % replicas},
            device_id_type=MESH,
        )
        copy.start()
        copies.append(copy)
    for copy in copies:
        copy.wait()


def exchange(values, replicas):
    return pl.pallas_call(
        functools.partial(exchange_kernel, replicas),
        out_shape=jax.ShapeDtypeStruct((replicas - 1,) + values.shape, values.dtype),
        in_specs=[VMEM],
        out_specs=VMEM,
        scratch_shapes=[
            pltpu.SemaphoreType.DMA((replicas - 1,)),
            pltpu.SemaphoreType.DMA((replicas - 1,)),
        ],
        compiler_params=pltpu.CompilerParams(collective_id=1, has_side_effects=True),
        name="exchange",
    )(values)


def scatter_kernel(size, parts, out, held, send, recv):
    me = lax.axis_index("tensor")
    greet("tensor", [(me + k) % size for k in range(1, size)])
    copies = []
    for k in range(1, size):
        target = (me + k) % size
        copy = pltpu.make_async_remote_copy(
            src_ref=parts.at[target],
            dst_ref=held.at[k - 1],
            send_sem=send.at[k - 1],
            recv_sem=recv.at[k - 1],
            device_id={"tensor": target},
            device_id_type=MESH,
        )
        copy.start()
        copies.append(copy)
    total = parts[me].astype(jnp.float32)
    for k in range(1, size):
        copies[k - 1].wait_recv()
        total = total + held[k - 1].astype(jnp.float32)
    out[...] = total.astype(out.dtype)
    for copy in copies:
        copy.wait_send()


def scatter_sum(parts):
    size = parts.shape[0]
    return pl.pallas_call(
        functools.partial(scatter_kernel, size),
        out_shape=jax.ShapeDtypeStruct(parts.shape[1:], parts.dtype),
        in_specs=[VMEM],
        out_specs=VMEM,
        scratch_shapes=[
            pltpu.VMEM((size - 1,) + parts.shape[1:], parts.dtype),
            pltpu.SemaphoreType.DMA((size - 1,)),
            pltpu.SemaphoreType.DMA((size - 1,)),
        ],
        compiler_params=pltpu.CompilerParams(collective_id=2, has_side_effects=True),
        name="scatter_sum",
    )(parts)


def dot(a, b):
    return jnp.dot(a, b, preferred_element_type=jnp.float32)


def contract(a, b, dim):
    return lax.dot_general(
        a, b, (((dim,), (dim,)), ((), ())), preferred_element_type=jnp.float32
    )


def lanes(shape):
    return lax.broadcasted_iota(jnp.int32, shape, 1) % TILE


def moment_kernel(
    chunk, hidden, grads, momentum, offsets, spread, row, col_high, col_low,
    inverse_row, inverse_col, kept, mine, sent,
):
    half = offsets.shape[0]
    place = lanes((half, chunk)).astype(jnp.float32)
    total = None
    for start in range(0, grads.shape[1], chunk):
        span = slice(start, start + chunk)
        moment = BETA_DECAY * momentum[0, :, span].astype(jnp.float32) + dot(
            hidden[...], grads[:, span]
        )
        rounded = moment.astype(jnp.bfloat16)
        mixed = dot(row[...], jnp.concatenate([rounded, rounded], axis=0)).astype(jnp.bfloat16)
        spectrum = dot(mixed, col_high[...]) + dot(mixed, col_low[...])
        offset = dot(offsets[...], spread[:, span])
        picked = jnp.where(
            offset == place,
            spectrum[:half],
            jnp.where(offset == place + TILE, spectrum[half:], 0.0),
        ).astype(jnp.bfloat16)
        values = contract(picked, spread[:, span], 1)
        total = values if total is None else total + values
        wide = dot(picked, inverse_col[...])
        odd = offset >= TILE
        pair = jnp.concatenate(
            [jnp.where(odd, 0.0, wide), jnp.where(odd, wide, 0.0)], axis=0
        ).astype(jnp.bfloat16)
        own = dot(inverse_row[...], pair)
        kept[0, :, span] = (moment - own).astype(jnp.bfloat16)
        mine[:, span] = own.astype(jnp.bfloat16)
    sent[...] = total.astype(jnp.bfloat16)


def whole_block(array):
    return pl.BlockSpec(array.shape, lambda i: (0,) * array.ndim)


def moment_pass(hidden, grads, momentum, offsets, spread, mats, strip, chunk):
    rows, breadth = momentum.shape[1:]
    tall = strip * TILE
    half = tall // 2
    columns = spread.shape[0]
    row, col_high, col_low, inverse_row, inverse_col = mats
    return pl.pallas_call(
        functools.partial(moment_kernel, chunk),
        grid=(rows // tall,),
        out_shape=(
            jax.ShapeDtypeStruct((1, rows, breadth), jnp.bfloat16),
            jax.ShapeDtypeStruct((rows, breadth), jnp.bfloat16),
            jax.ShapeDtypeStruct((rows // 2, columns), jnp.bfloat16),
        ),
        in_specs=[
            pl.BlockSpec((tall, hidden.shape[1]), lambda i: (i, 0)),
            whole_block(grads),
            pl.BlockSpec((1, tall, breadth), lambda i: (0, i, 0)),
            pl.BlockSpec((half, columns), lambda i: (i, 0)),
            whole_block(spread),
            whole_block(row),
            whole_block(col_high),
            whole_block(col_low),
            whole_block(inverse_row),
            whole_block(inverse_col),
        ],
        out_specs=(
            pl.BlockSpec((1, tall, breadth), lambda i: (0, i, 0)),
            pl.BlockSpec((tall, breadth), lambda i: (i, 0)),
            pl.BlockSpec((half, columns), lambda i: (i, 0)),
        ),
        name="moment_pass",
    )(hidden, grads, momentum, offsets, spread, row, col_high, col_low, inverse_row, inverse_col)


def output_kernel(
    chunk, replicas, hidden, down, mine, values, offsets, spread, inverse_row, inverse_col,
    out, total,
):
    step = pl.program_id(0)
    half = offsets.shape[1]
    place = lanes((half, chunk)).astype(jnp.float32)

    @pl.when(step == 0)
    def _():
        total[...] = jnp.zeros_like(total)

    for start in range(0, down.shape[1], chunk):
        span = slice(start, start + chunk)
        even = odd = 0.0
        for k in range(replicas - 1):
            offset = dot(offsets[k], spread[:, span])
            value = dot(values[k], spread[:, span])
            even = even + jnp.where(offset == place, value, 0.0)
            odd = odd + jnp.where(offset == place + TILE, value, 0.0)
        placed = jnp.concatenate([even, odd], axis=0).astype(jnp.bfloat16)
        wide = dot(placed, inverse_col[...]).astype(jnp.bfloat16)
        update = mine[:, span].astype(jnp.float32) + dot(inverse_row[...], wide)
        new = down[:, span].astype(jnp.float32) - (STEP_RATE / replicas) * update
        total[:, span] += contract(hidden[...], new.astype(jnp.bfloat16), 0)

    @pl.when(step == pl.num_programs(0) - 1)
    def _():
        out[...] = total[...].astype(out.dtype)


def output_pass(hidden, down, mine, values, offsets, spread, mats, strip, chunk, replicas):
    rows, breadth = down.shape
    tall = strip * TILE
    half = tall // 2
    columns = spread.shape[0]
    count = hidden.shape[1]
    inverse_row, inverse_col = mats[3:]
    return pl.pallas_call(
        functools.partial(output_kernel, chunk, replicas),
        grid=(rows // tall,),
        out_shape=jax.ShapeDtypeStruct((count, breadth), jnp.bfloat16),
        in_specs=[
            pl.BlockSpec((tall, count), lambda i: (i, 0)),
            pl.BlockSpec((tall, breadth), lambda i: (i, 0)),
            pl.BlockSpec((tall, breadth), lambda i: (i, 0)),
            pl.BlockSpec((replicas - 1, half, columns), lambda i: (0, i, 0)),
            pl.BlockSpec((replicas - 1, half, columns), lambda i: (0, i, 0)),
            whole_block(spread),
            whole_block(inverse_row),
            whole_block(inverse_col),
        ],
        out_specs=pl.BlockSpec((count, breadth), lambda i: (0, 0)),
        scratch_shapes=[pltpu.VMEM((count, breadth), jnp.float32)],
        name="output_pass",
    )(hidden, down, mine, values, offsets, spread, inverse_row, inverse_col)


def on_device(
    tokens, next_tokens, cotangent, gate_weight, up_weight, down_weight, momentum, indices
):
    size = lax.axis_size("tensor")
    replicas = lax.axis_size("replica")
    replica = lax.axis_index("replica")
    count, share = tokens.shape
    nexts = next_tokens.shape[0]
    breadth = share * size
    tile_rows, tile_cols, keep = indices.shape[1:]
    strip = next(n for n in (4, 2, 1) if tile_rows % n == 0)
    chunk = next(n for n in (256, 128) if breadth % n == 0)

    turned = next_tokens.T
    block = jnp.concatenate(
        [
            cotangent.T,
            tokens.T,
            jnp.concatenate([turned[: share // 2], turned[share // 2 :]], axis=1),
        ],
        axis=0,
    )
    gathered = gather_blocks(block, size)
    grads = gathered[:, :share].reshape(breadth, count).T
    features = gathered[:, share : 2 * share].reshape(breadth, count)
    tail = gathered[:, 2 * share :]
    next_features = jnp.concatenate([tail[:, :, :nexts], tail[:, :, nexts:]], axis=1)
    features = jnp.concatenate([features, next_features.reshape(breadth, nexts)], axis=1)
    gate = contract(gate_weight, features, 0)
    upper = contract(up_weight, features, 0)
    hidden = (jax.nn.silu(gate) * upper).astype(jnp.bfloat16)

    stride = TILE * TILE // keep
    offsets = indices - jnp.arange(keep, dtype=jnp.int32) * stride
    offsets = jnp.swapaxes(offsets.astype(jnp.bfloat16), 2, 3)
    offsets = offsets.reshape(replicas, tile_rows * keep, tile_cols)
    spread = jnp.asarray(np.kron(np.eye(tile_cols), np.ones((1, TILE))), jnp.bfloat16)
    mats = tables(strip, chunk)
    own_offsets = lax.dynamic_index_in_dim(offsets, replica, 0, keepdims=False)
    kept, mine, sent = moment_pass(
        hidden[:, :count], grads, momentum, own_offsets, spread, mats, strip, chunk
    )
    values = exchange(sent, replicas)
    other_offsets = jnp.stack(
        [
            lax.dynamic_index_in_dim(offsets, (replica + k) % replicas, 0, keepdims=False)
            for k in range(1, replicas)
        ]
    )
    partial = output_pass(
        hidden[:, count:], down_weight, mine, values, other_offsets, spread, mats, strip, chunk,
        replicas,
    )
    output = scatter_sum(partial.reshape(size, nexts // size, breadth))
    return (output, kept)


def solution(mesh):
    return jax.shard_map(
        on_device,
        mesh=mesh,
        in_specs=(
            P("replica", "tensor"),
            P("replica", "tensor"),
            P("replica", "tensor"),
            P(None, "tensor"),
            P(None, "tensor"),
            P("tensor", None),
            P("replica", "tensor", None),
            P(None, "tensor", None, None),
        ),
        out_specs=(P(("replica", "tensor"), None), P("replica", "tensor", None)),
        check_vma=False,
    )
```

```python
import functools

import jax
import jax.numpy as jnp
import numpy as np
from jax import lax
from jax.experimental import pallas as pl
from jax.experimental.pallas import tpu as pltpu
from jax.sharding import PartitionSpec as P

TILE = 64
BETA_DECAY = 0.9
STEP_RATE = 0.1
MESH = pl.DeviceIdType.MESH
VMEM = pl.BlockSpec(memory_space=pltpu.VMEM)


def cosine_table():
    freq = np.arange(TILE)[:, None]
    place = np.arange(TILE)[None, :]
    table = np.cos(np.pi * (2.0 * place + 1.0) * freq / (2.0 * TILE))
    return table * np.where(freq == 0, np.sqrt(1.0 / TILE), np.sqrt(2.0 / TILE))


def split_bf16(table):
    high = jnp.asarray(table, jnp.float32).astype(jnp.bfloat16)
    rest = jnp.asarray(table, jnp.float32) - high.astype(jnp.float32)
    return high, rest.astype(jnp.bfloat16)


def tables(strip, chunk):
    table = cosine_table()
    across = np.kron(np.eye(chunk // TILE), table)
    down = np.concatenate(
        [np.kron(np.eye(strip), table[0::2]), np.kron(np.eye(strip), table[1::2])], axis=0
    )
    row_high, row_low = split_bf16(down)
    col_high, col_low = split_bf16(across.T)
    row = jnp.concatenate([row_high, row_low], axis=1)
    inverse_row = jnp.asarray(down.T, jnp.float32).astype(jnp.bfloat16)
    inverse_col = jnp.asarray(across, jnp.float32).astype(jnp.bfloat16)
    return row, col_high, col_low, inverse_row, inverse_col


def flip(index, bits):
    bit = 1
    while bit <= bits:
        if bits & bit:
            index = index + bit - 2 * bit * ((index // bit) % 2)
        bit *= 2
    return index


def greet(axis, others):
    barrier = pltpu.get_barrier_semaphore()
    for other in others:
        pl.semaphore_signal(barrier, inc=1, device_id={axis: other}, device_id_type=MESH)
    pl.semaphore_wait(barrier, len(others))


def gather_kernel(size, block, out, send, recv, local):
    me = lax.axis_index("tensor")
    depth = size // 4
    z, x, core = me // 4, (me // 2) % 2, me % 2

    def slot(zz, xx, cc):
        return (zz * 2 + xx) * 2 + cc

    others = [flip(z, k) for k in range(1, depth)]
    side, twin = slot(z, 1 - x, core), slot(z, x, 1 - core)
    greet("tensor", [slot(zz, x, core) for zz in others] + [side, twin])
    own = pltpu.make_async_copy(block, out.at[me], local)
    own.start()
    copies = []

    def push(source, which, target):
        copy = pltpu.make_async_remote_copy(
            src_ref=source,
            dst_ref=out.at[which],
            send_sem=send.at[len(copies)],
            recv_sem=recv.at[which],
            device_id={"tensor": target},
            device_id_type=MESH,
        )
        copy.start()
        copies.append(copy)

    def arrive(which):
        pltpu.make_async_remote_copy(
            src_ref=block,
            dst_ref=out.at[which],
            send_sem=send.at[0],
            recv_sem=recv.at[which],
            device_id={"tensor": twin},
            device_id_type=MESH,
        ).wait_recv()

    push(block, me, side)
    for zz in others:
        push(block, me, slot(zz, x, core))
    push(block, me, twin)
    for zz in others:
        which = slot(zz, x, core)
        arrive(which)
        push(out.at[which], which, side)
        push(out.at[which], which, twin)
    for zz in [z] + others:
        which = slot(zz, 1 - x, core)
        arrive(which)
        push(out.at[which], which, twin)
    for zz in [z] + others:
        arrive(slot(zz, x, 1 - core))
        arrive(slot(zz, 1 - x, 1 - core))
    own.wait()
    for copy in copies:
        copy.wait_send()


def gather_blocks(block, size):
    return pl.pallas_call(
        functools.partial(gather_kernel, size),
        out_shape=jax.ShapeDtypeStruct((size,) + block.shape, block.dtype),
        in_specs=[VMEM],
        out_specs=VMEM,
        scratch_shapes=[
            pltpu.SemaphoreType.DMA((size,)),
            pltpu.SemaphoreType.DMA((size,)),
            pltpu.SemaphoreType.DMA,
        ],
        compiler_params=pltpu.CompilerParams(collective_id=0, has_side_effects=True),
        name="gather_blocks",
    )(block)


def exchange_kernel(replicas, values, out, send, recv):
    me = lax.axis_index("replica")
    greet("replica", [(me + k) % replicas for k in range(1, replicas)])
    copies = []
    for k in range(1, replicas):
        copy = pltpu.make_async_remote_copy(
            src_ref=values,
            dst_ref=out.at[k - 1],
            send_sem=send.at[k - 1],
            recv_sem=recv.at[k - 1],
            device_id={"replica": (me - k + replicas) % replicas},
            device_id_type=MESH,
        )
        copy.start()
        copies.append(copy)
    for copy in copies:
        copy.wait()


def exchange(values, replicas):
    return pl.pallas_call(
        functools.partial(exchange_kernel, replicas),
        out_shape=jax.ShapeDtypeStruct((replicas - 1,) + values.shape, values.dtype),
        in_specs=[VMEM],
        out_specs=VMEM,
        scratch_shapes=[
            pltpu.SemaphoreType.DMA((replicas - 1,)),
            pltpu.SemaphoreType.DMA((replicas - 1,)),
        ],
        compiler_params=pltpu.CompilerParams(collective_id=1, has_side_effects=True),
        name="exchange",
    )(values)


def scatter_kernel(size, parts, out, held, send, recv):
    me = lax.axis_index("tensor")
    greet("tensor", [(me + k) % size for k in range(1, size)])
    copies = []
    for k in range(1, size):
        target = (me + k) % size
        copy = pltpu.make_async_remote_copy(
            src_ref=parts.at[target],
            dst_ref=held.at[k - 1],
            send_sem=send.at[k - 1],
            recv_sem=recv.at[k - 1],
            device_id={"tensor": target},
            device_id_type=MESH,
        )
        copy.start()
        copies.append(copy)
    total = parts[me].astype(jnp.float32)
    for k in range(1, size):
        copies[k - 1].wait_recv()
        total = total + held[k - 1].astype(jnp.float32)
    out[...] = total.astype(out.dtype)
    for copy in copies:
        copy.wait_send()


def scatter_sum(parts):
    size = parts.shape[0]
    return pl.pallas_call(
        functools.partial(scatter_kernel, size),
        out_shape=jax.ShapeDtypeStruct(parts.shape[1:], parts.dtype),
        in_specs=[VMEM],
        out_specs=VMEM,
        scratch_shapes=[
            pltpu.VMEM((size - 1,) + parts.shape[1:], parts.dtype),
            pltpu.SemaphoreType.DMA((size - 1,)),
            pltpu.SemaphoreType.DMA((size - 1,)),
        ],
        compiler_params=pltpu.CompilerParams(collective_id=2, has_side_effects=True),
        name="scatter_sum",
    )(parts)


def dot(a, b):
    return jnp.dot(a, b, preferred_element_type=jnp.float32)


def contract(a, b, dim):
    return lax.dot_general(
        a, b, (((dim,), (dim,)), ((), ())), preferred_element_type=jnp.float32
    )


def lanes(shape):
    return lax.broadcasted_iota(jnp.int32, shape, 1) % TILE


def strip_offsets(indices, which):
    strip, columns, keep = indices.shape[1:]
    first = lax.broadcasted_iota(jnp.int32, (columns, keep), 1) * (TILE * TILE // keep)
    listed = [
        (indices[which, n] - first).astype(jnp.float32).astype(jnp.bfloat16) for n in range(strip)
    ]
    return jnp.concatenate(listed, axis=1)


def moment_kernel(
    chunk, hidden, grads, momentum, indices, spread, gather, row, col_high, col_low,
    inverse_row, inverse_col, kept, mine, sent,
    moment, mixed, offset, picked, stacked, pair,
):
    tall, breadth = moment.shape
    half = tall // 2
    spans = [slice(start, start + chunk) for start in range(0, breadth, chunk)]
    own_offsets = strip_offsets(indices, lax.axis_index("replica"))
    for span in spans:
        offset[:, span] = contract(own_offsets, spread[:, span], 0)
    for span in spans:
        moment[:, span] = BETA_DECAY * momentum[0, :, span].astype(jnp.float32) + contract(
            hidden[...], grads[span, :], 1
        )
    for k, span in enumerate(spans):
        rounded = moment[:, span].astype(jnp.bfloat16)
        mixed[k * tall : (k + 1) * tall] = dot(
            row[...], jnp.concatenate([rounded, rounded], axis=0)
        ).astype(jnp.bfloat16)
    place = lanes((half, chunk)).astype(jnp.float32)
    for k, span in enumerate(spans):
        part = mixed[k * tall : (k + 1) * tall]
        spectrum = dot(part, col_high[...]) + dot(part, col_low[...])
        where = offset[:, span]
        values = jnp.where(
            where == place,
            spectrum[:half],
            jnp.where(where == place + TILE, spectrum[half:], 0.0),
        ).astype(jnp.bfloat16)
        picked[:, span] = values
        stacked[k * half : (k + 1) * half] = values
    sent[...] = dot(picked[...], gather[...]).astype(jnp.bfloat16)
    for k, span in enumerate(spans):
        wide = dot(stacked[k * half : (k + 1) * half], inverse_col[...])
        odd = offset[:, span] >= TILE
        pair[:half, span] = jnp.where(odd, 0.0, wide).astype(jnp.bfloat16)
        pair[half:, span] = jnp.where(odd, wide, 0.0).astype(jnp.bfloat16)
    for span in spans:
        own = dot(inverse_row[...], pair[:, span])
        kept[0, :, span] = (moment[:, span] - own).astype(jnp.bfloat16)
        mine[:, span] = own.astype(jnp.bfloat16)


def whole_block(array):
    return pl.BlockSpec(array.shape, lambda i: (0,) * array.ndim)


def moment_pass(hidden, grads, momentum, indices, spread, mats, strip, chunk):
    rows, breadth = momentum.shape[1:]
    tall = strip * TILE
    replicas, _, columns, keep = indices.shape
    half = strip * keep
    row, col_high, col_low, inverse_row, inverse_col = mats
    gather = spread.T
    return pl.pallas_call(
        functools.partial(moment_kernel, chunk),
        grid=(rows // tall,),
        out_shape=(
            jax.ShapeDtypeStruct((1, rows, breadth), jnp.bfloat16),
            jax.ShapeDtypeStruct((rows, breadth), jnp.bfloat16),
            jax.ShapeDtypeStruct((rows // 2, columns), jnp.bfloat16),
        ),
        in_specs=[
            pl.BlockSpec((tall, hidden.shape[1]), lambda i: (i, 0)),
            whole_block(grads),
            pl.BlockSpec((1, tall, breadth), lambda i: (0, i, 0)),
            pl.BlockSpec((replicas, strip, columns, keep), lambda i: (0, i, 0, 0)),
            whole_block(spread),
            whole_block(gather),
            whole_block(row),
            whole_block(col_high),
            whole_block(col_low),
            whole_block(inverse_row),
            whole_block(inverse_col),
        ],
        out_specs=(
            pl.BlockSpec((1, tall, breadth), lambda i: (0, i, 0)),
            pl.BlockSpec((tall, breadth), lambda i: (i, 0)),
            pl.BlockSpec((half, columns), lambda i: (i, 0)),
        ),
        scratch_shapes=[
            pltpu.VMEM((tall, breadth), jnp.float32),
            pltpu.VMEM((tall * (breadth // chunk), chunk), jnp.bfloat16),
            pltpu.VMEM((half, breadth), jnp.float32),
            pltpu.VMEM((half, breadth), jnp.bfloat16),
            pltpu.VMEM((half * (breadth // chunk), chunk), jnp.bfloat16),
            pltpu.VMEM((tall, breadth), jnp.bfloat16),
        ],
        name="moment_pass",
    )(
        hidden, grads, momentum, indices, spread, gather, row, col_high, col_low, inverse_row,
        inverse_col,
    )


def output_kernel(
    chunk, hidden, down, mine, values, indices, spread, inverse_row, inverse_col,
    out, total, placed, wide, new,
):
    step = pl.program_id(0)
    replicas, strip, _, keep = indices.shape
    half = strip * keep
    tall, breadth = new.shape
    spans = [slice(start, start + chunk) for start in range(0, breadth, chunk)]
    replica = lax.axis_index("replica")

    @pl.when(step == 0)
    def _():
        total[...] = jnp.zeros_like(total)

    place = lanes((half, chunk)).astype(jnp.float32)
    listed = [
        strip_offsets(indices, (replica + k) % replicas) for k in range(1, replicas)
    ]
    for n, span in enumerate(spans):
        even = odd = 0.0
        for k in range(replicas - 1):
            offset = contract(listed[k], spread[:, span], 0)
            value = dot(values[k], spread[:, span])
            even = even + jnp.where(offset == place, value, 0.0)
            odd = odd + jnp.where(offset == place + TILE, value, 0.0)
        placed[n * tall : n * tall + half] = even.astype(jnp.bfloat16)
        placed[n * tall + half : (n + 1) * tall] = odd.astype(jnp.bfloat16)
    for n, span in enumerate(spans):
        wide[:, span] = dot(placed[n * tall : (n + 1) * tall], inverse_col[...]).astype(
            jnp.bfloat16
        )
    for span in spans:
        update = mine[:, span].astype(jnp.float32) + dot(inverse_row[...], wide[:, span])
        new[:, span] = (
            down[:, span].astype(jnp.float32) - (STEP_RATE / replicas) * update
        ).astype(jnp.bfloat16)
    for span in spans:
        total[:, span] += contract(hidden[...], new[:, span], 0)

    @pl.when(step == pl.num_programs(0) - 1)
    def _():
        size, rows, _ = out.shape
        for n in range(size):
            out[n] = total[n * rows : (n + 1) * rows].astype(out.dtype)


def output_pass(hidden, down, mine, values, indices, spread, mats, strip, chunk, size):
    rows, breadth = down.shape
    tall = strip * TILE
    replicas, _, columns, keep = indices.shape
    half = strip * keep
    count = hidden.shape[1]
    inverse_row, inverse_col = mats[3:]
    return pl.pallas_call(
        functools.partial(output_kernel, chunk),
        grid=(rows // tall,),
        out_shape=jax.ShapeDtypeStruct((size, count // size, breadth), jnp.bfloat16),
        in_specs=[
            pl.BlockSpec((tall, count), lambda i: (i, 0)),
            pl.BlockSpec((tall, breadth), lambda i: (i, 0)),
            pl.BlockSpec((tall, breadth), lambda i: (i, 0)),
            pl.BlockSpec((replicas - 1, half, columns), lambda i: (0, i, 0)),
            pl.BlockSpec((replicas, strip, columns, keep), lambda i: (0, i, 0, 0)),
            whole_block(spread),
            whole_block(inverse_row),
            whole_block(inverse_col),
        ],
        out_specs=pl.BlockSpec((size, count // size, breadth), lambda i: (0, 0, 0)),
        scratch_shapes=[
            pltpu.VMEM((count, breadth), jnp.float32),
            pltpu.VMEM((tall * (breadth // chunk), chunk), jnp.bfloat16),
            pltpu.VMEM((tall, breadth), jnp.bfloat16),
            pltpu.VMEM((tall, breadth), jnp.bfloat16),
        ],
        name="output_pass",
    )(hidden, down, mine, values, indices, spread, inverse_row, inverse_col)


def on_device(
    tokens, next_tokens, cotangent, gate_weight, up_weight, down_weight, momentum, indices
):
    size = lax.axis_size("tensor")
    replicas = lax.axis_size("replica")
    count, share = tokens.shape
    nexts = next_tokens.shape[0]
    breadth = share * size
    tile_rows, tile_cols, keep = indices.shape[1:]
    strip = next(n for n in (4, 2, 1) if tile_rows % n == 0)
    chunk = next(n for n in (256, 128) if breadth % n == 0)

    turned = next_tokens.T
    block = jnp.concatenate(
        [
            cotangent.T,
            tokens.T,
            jnp.concatenate([turned[: share // 2], turned[share // 2 :]], axis=1),
        ],
        axis=0,
    )
    gathered = gather_blocks(block, size)
    grads = gathered[:, :share].reshape(breadth, count)
    features = gathered[:, share : 2 * share].reshape(breadth, count)
    tail = gathered[:, 2 * share :]
    next_features = jnp.concatenate([tail[:, :, :nexts], tail[:, :, nexts:]], axis=1)
    features = jnp.concatenate([features, next_features.reshape(breadth, nexts)], axis=1)
    gate = contract(gate_weight, features, 0)
    upper = contract(up_weight, features, 0)
    hidden = (jax.nn.silu(gate) * upper).astype(jnp.bfloat16)

    spread = jnp.asarray(np.kron(np.eye(tile_cols), np.ones((1, TILE))), jnp.bfloat16)
    mats = tables(strip, chunk)
    kept, mine, sent = moment_pass(
        hidden[:, :count], grads, momentum, indices, spread, mats, strip, chunk
    )
    values = exchange(sent, replicas)
    partial = output_pass(
        hidden[:, count:], down_weight, mine, values, indices, spread, mats, strip, chunk, size
    )
    output = scatter_sum(partial)
    return (output, kept)


def solution(mesh):
    return jax.shard_map(
        on_device,
        mesh=mesh,
        in_specs=(
            P("replica", "tensor"),
            P("replica", "tensor"),
            P("replica", "tensor"),
            P(None, "tensor"),
            P(None, "tensor"),
            P("tensor", None),
            P("replica", "tensor", None),
            P(None, "tensor", None, None),
        ),
        out_specs=(P(("replica", "tensor"), None), P("replica", "tensor", None)),
        check_vma=False,
    )
```

```python
import functools

import jax
import jax.numpy as jnp
import numpy as np
from jax import lax
from jax.experimental import pallas as pl
from jax.experimental.pallas import tpu as pltpu
from jax.sharding import PartitionSpec as P

TILE = 64
BETA_DECAY = 0.9
STEP_RATE = 0.1
MESH = pl.DeviceIdType.MESH
VMEM = pl.BlockSpec(memory_space=pltpu.VMEM)


def cosine_table():
    freq = np.arange(TILE)[:, None]
    place = np.arange(TILE)[None, :]
    table = np.cos(np.pi * (2.0 * place + 1.0) * freq / (2.0 * TILE))
    return table * np.where(freq == 0, np.sqrt(1.0 / TILE), np.sqrt(2.0 / TILE))


def split_bf16(table):
    high = jnp.asarray(table, jnp.float32).astype(jnp.bfloat16)
    rest = jnp.asarray(table, jnp.float32) - high.astype(jnp.float32)
    return high, rest.astype(jnp.bfloat16)


def tables(strip, chunk):
    table = cosine_table()
    across = np.kron(np.eye(chunk // TILE), table)
    down = np.concatenate(
        [np.kron(np.eye(strip), table[0::2]), np.kron(np.eye(strip), table[1::2])], axis=0
    )
    row_high, row_low = split_bf16(down)
    col_high, col_low = split_bf16(across.T)
    row = jnp.concatenate([row_high, row_low], axis=1)
    inverse_row = jnp.asarray(down.T, jnp.float32).astype(jnp.bfloat16)
    inverse_col = jnp.asarray(across, jnp.float32).astype(jnp.bfloat16)
    return row, col_high, col_low, inverse_row, inverse_col


def flip(index, bits):
    bit = 1
    while bit <= bits:
        if bits & bit:
            index = index + bit - 2 * bit * ((index // bit) % 2)
        bit *= 2
    return index


def greet(axis, others):
    barrier = pltpu.get_barrier_semaphore()
    for other in others:
        pl.semaphore_signal(barrier, inc=1, device_id={axis: other}, device_id_type=MESH)
    pl.semaphore_wait(barrier, len(others))


def hidden_kernel(
    size, feature_block, grad_block, gate_weight, up_weight, grads, hidden, next_hidden,
    held, features, turned, gate, upper, send, recv, local,
):
    me = lax.axis_index("tensor")
    depth = size // 4
    z, x, core = me // 4, (me // 2) % 2, me % 2
    blocks, kept = (feature_block, grad_block), (held, grads)

    def slot(zz, xx, cc):
        return (zz * 2 + xx) * 2 + cc

    loads = [
        pltpu.make_async_copy(source, target, local.at[n])
        for n, (source, target) in enumerate(
            [
                (feature_block, held.at[me]),
                (grad_block, grads.at[me]),
                (gate_weight, gate),
                (up_weight, upper),
            ]
        )
    ]
    for load in loads:
        load.start()
    others = [flip(z, k) for k in range(1, depth)]
    side, twin = slot(z, 1 - x, core), slot(z, x, 1 - core)
    greet("tensor", [slot(zz, x, core) for zz in others] + [side, twin])
    copies = []

    def push(kind, which, target, source=None):
        copy = pltpu.make_async_remote_copy(
            src_ref=kept[kind].at[which] if source is None else source,
            dst_ref=kept[kind].at[which],
            send_sem=send.at[len(copies)],
            recv_sem=recv.at[kind, which],
            device_id={"tensor": target},
            device_id_type=MESH,
        )
        copy.start()
        copies.append(copy)

    def arrive(kind, which):
        pltpu.make_async_remote_copy(
            src_ref=blocks[kind],
            dst_ref=kept[kind].at[which],
            send_sem=send.at[0],
            recv_sem=recv.at[kind, which],
            device_id={"tensor": twin},
            device_id_type=MESH,
        ).wait_recv()

    for kind in range(2):
        for target in [side] + [slot(zz, x, core) for zz in others] + [twin]:
            push(kind, me, target, blocks[kind])
    for kind in range(2):
        for zz in others:
            which = slot(zz, x, core)
            arrive(kind, which)
            push(kind, which, side)
            push(kind, which, twin)
    for kind in range(2):
        for zz in [z] + others:
            which = slot(zz, 1 - x, core)
            arrive(kind, which)
            push(kind, which, twin)
    for load in loads:
        load.wait()
    for zz in [z] + others:
        arrive(0, slot(zz, x, 1 - core))
        arrive(0, slot(zz, 1 - x, 1 - core))
    share, count = grads.shape[1:]
    nexts = next_hidden.shape[1]
    split = share // 2
    for n in range(size):
        base = n * share
        features[base : base + share, :count] = held[n, :share]
        features[base : base + split, count:] = held[n, share:, :nexts]
        features[base + split : base + share, count:] = held[n, share:, nexts:]
    turned[...] = features[...].T
    wide = dot(turned[...], gate[...])
    mixed = (wide / (1.0 + jnp.exp(-wide)) * dot(turned[...], upper[...])).astype(jnp.bfloat16).T
    hidden[...] = mixed[:, :count]
    next_hidden[...] = mixed[:, count:]
    for zz in [z] + others:
        arrive(1, slot(zz, x, 1 - core))
        arrive(1, slot(zz, 1 - x, 1 - core))
    for copy in copies:
        copy.wait_send()


def hidden_pass(feature_block, grad_block, gate_weight, up_weight, nexts, size):
    share, count = grad_block.shape
    breadth, width = gate_weight.shape
    kind = jnp.bfloat16
    hbm = pl.BlockSpec(memory_space=pl.ANY)
    return pl.pallas_call(
        functools.partial(hidden_kernel, size),
        out_shape=(
            jax.ShapeDtypeStruct((size, share, count), kind),
            jax.ShapeDtypeStruct((width, count), kind),
            jax.ShapeDtypeStruct((width, nexts), kind),
        ),
        in_specs=[VMEM, VMEM, hbm, hbm],
        out_specs=(VMEM, VMEM, VMEM),
        scratch_shapes=[
            pltpu.VMEM((size,) + feature_block.shape, kind),
            pltpu.VMEM((breadth, count + nexts), kind),
            pltpu.VMEM((count + nexts, breadth), kind),
            pltpu.VMEM(gate_weight.shape, kind),
            pltpu.VMEM(up_weight.shape, kind),
            pltpu.SemaphoreType.DMA((2 * size,)),
            pltpu.SemaphoreType.DMA((2, size)),
            pltpu.SemaphoreType.DMA((4,)),
        ],
        compiler_params=pltpu.CompilerParams(collective_id=0, has_side_effects=True),
        name="hidden_pass",
    )(feature_block, grad_block, gate_weight, up_weight)


def exchange_kernel(replicas, values, out, send, recv):
    me = lax.axis_index("replica")
    greet("replica", [(me + k) % replicas for k in range(1, replicas)])
    copies = []
    for k in range(1, replicas):
        copy = pltpu.make_async_remote_copy(
            src_ref=values,
            dst_ref=out.at[k - 1],
            send_sem=send.at[k - 1],
            recv_sem=recv.at[k - 1],
            device_id={"replica": (me - k + replicas) % replicas},
            device_id_type=MESH,
        )
        copy.start()
        copies.append(copy)
    for copy in copies:
        copy.wait()


def exchange(values, replicas):
    return pl.pallas_call(
        functools.partial(exchange_kernel, replicas),
        out_shape=jax.ShapeDtypeStruct((replicas - 1,) + values.shape, values.dtype),
        in_specs=[VMEM],
        out_specs=VMEM,
        scratch_shapes=[
            pltpu.SemaphoreType.DMA((replicas - 1,)),
            pltpu.SemaphoreType.DMA((replicas - 1,)),
        ],
        compiler_params=pltpu.CompilerParams(collective_id=1, has_side_effects=True),
        name="exchange",
    )(values)


def scatter_kernel(size, parts, out, held, send, recv):
    me = lax.axis_index("tensor")
    greet("tensor", [(me + k) % size for k in range(1, size)])
    copies = []
    for k in range(1, size):
        target = (me + k) % size
        copy = pltpu.make_async_remote_copy(
            src_ref=parts.at[target],
            dst_ref=held.at[k - 1],
            send_sem=send.at[k - 1],
            recv_sem=recv.at[k - 1],
            device_id={"tensor": target},
            device_id_type=MESH,
        )
        copy.start()
        copies.append(copy)
    total = parts[me].astype(jnp.float32)
    for k in range(1, size):
        copies[k - 1].wait_recv()
        total = total + held[k - 1].astype(jnp.float32)
    out[...] = total.astype(out.dtype)
    for copy in copies:
        copy.wait_send()


def scatter_sum(parts):
    size = parts.shape[0]
    return pl.pallas_call(
        functools.partial(scatter_kernel, size),
        out_shape=jax.ShapeDtypeStruct(parts.shape[1:], parts.dtype),
        in_specs=[VMEM],
        out_specs=VMEM,
        scratch_shapes=[
            pltpu.VMEM((size - 1,) + parts.shape[1:], parts.dtype),
            pltpu.SemaphoreType.DMA((size - 1,)),
            pltpu.SemaphoreType.DMA((size - 1,)),
        ],
        compiler_params=pltpu.CompilerParams(collective_id=2, has_side_effects=True),
        name="scatter_sum",
    )(parts)


def dot(a, b):
    return jnp.dot(a, b, preferred_element_type=jnp.float32)


def contract(a, b, dim):
    return lax.dot_general(
        a, b, (((dim,), (dim,)), ((), ())), preferred_element_type=jnp.float32
    )


def lanes(shape):
    return lax.broadcasted_iota(jnp.int32, shape, 1) % TILE


def strip_offsets(indices, which):
    strip, keep, columns = indices.shape[1:]
    first = lax.broadcasted_iota(jnp.int32, (keep, columns), 0) * (TILE * TILE // keep)
    listed = [
        (indices[which, n] - first).astype(jnp.float32).astype(jnp.bfloat16) for n in range(strip)
    ]
    return jnp.concatenate(listed, axis=0)


def moment_kernel(
    chunk, hidden, grads, momentum, indices, spread, gather, row, col_high, col_low,
    inverse_row, inverse_col, kept, mine, sent,
    moment, mixed, offset, picked, stacked, pair,
):
    tall, breadth = moment.shape
    half = tall // 2
    spans = [slice(start, start + chunk) for start in range(0, breadth, chunk)]
    own_offsets = strip_offsets(indices, lax.axis_index("replica"))
    for span in spans:
        offset[:, span] = dot(own_offsets, spread[:, span])
    for span in spans:
        moment[:, span] = BETA_DECAY * momentum[0, :, span].astype(jnp.float32) + contract(
            hidden[...], grads[span, :], 1
        )
    for k, span in enumerate(spans):
        rounded = moment[:, span].astype(jnp.bfloat16)
        mixed[k * tall : (k + 1) * tall] = dot(
            row[...], jnp.concatenate([rounded, rounded], axis=0)
        ).astype(jnp.bfloat16)
    place = lanes((half, chunk)).astype(jnp.float32)
    for k, span in enumerate(spans):
        part = mixed[k * tall : (k + 1) * tall]
        spectrum = dot(part, col_high[...]) + dot(part, col_low[...])
        where = offset[:, span]
        values = jnp.where(
            where == place,
            spectrum[:half],
            jnp.where(where == place + TILE, spectrum[half:], 0.0),
        ).astype(jnp.bfloat16)
        picked[:, span] = values
        stacked[k * half : (k + 1) * half] = values
    sent[...] = dot(picked[...], gather[...]).astype(jnp.bfloat16)
    for k, span in enumerate(spans):
        wide = dot(stacked[k * half : (k + 1) * half], inverse_col[...])
        odd = offset[:, span] >= TILE
        pair[:half, span] = jnp.where(odd, 0.0, wide).astype(jnp.bfloat16)
        pair[half:, span] = jnp.where(odd, wide, 0.0).astype(jnp.bfloat16)
    for span in spans:
        own = dot(inverse_row[...], pair[:, span])
        kept[0, :, span] = (moment[:, span] - own).astype(jnp.bfloat16)
        mine[:, span] = own.astype(jnp.bfloat16)


def whole_block(array):
    return pl.BlockSpec(array.shape, lambda i: (0,) * array.ndim)


def moment_pass(hidden, grads, momentum, indices, spread, mats, strip, chunk):
    rows, breadth = momentum.shape[1:]
    tall = strip * TILE
    replicas, _, keep, columns = indices.shape
    half = strip * keep
    row, col_high, col_low, inverse_row, inverse_col = mats
    gather = spread.T
    return pl.pallas_call(
        functools.partial(moment_kernel, chunk),
        grid=(rows // tall,),
        out_shape=(
            jax.ShapeDtypeStruct((1, rows, breadth), jnp.bfloat16),
            jax.ShapeDtypeStruct((rows, breadth), jnp.bfloat16),
            jax.ShapeDtypeStruct((rows // 2, columns), jnp.bfloat16),
        ),
        in_specs=[
            pl.BlockSpec((tall, hidden.shape[1]), lambda i: (i, 0)),
            whole_block(grads),
            pl.BlockSpec((1, tall, breadth), lambda i: (0, i, 0)),
            pl.BlockSpec((replicas, strip, keep, columns), lambda i: (0, i, 0, 0)),
            whole_block(spread),
            whole_block(gather),
            whole_block(row),
            whole_block(col_high),
            whole_block(col_low),
            whole_block(inverse_row),
            whole_block(inverse_col),
        ],
        out_specs=(
            pl.BlockSpec((1, tall, breadth), lambda i: (0, i, 0)),
            pl.BlockSpec((tall, breadth), lambda i: (i, 0)),
            pl.BlockSpec((half, columns), lambda i: (i, 0)),
        ),
        scratch_shapes=[
            pltpu.VMEM((tall, breadth), jnp.float32),
            pltpu.VMEM((tall * (breadth // chunk), chunk), jnp.bfloat16),
            pltpu.VMEM((half, breadth), jnp.float32),
            pltpu.VMEM((half, breadth), jnp.bfloat16),
            pltpu.VMEM((half * (breadth // chunk), chunk), jnp.bfloat16),
            pltpu.VMEM((tall, breadth), jnp.bfloat16),
        ],
        name="moment_pass",
    )(
        hidden, grads, momentum, indices, spread, gather, row, col_high, col_low, inverse_row,
        inverse_col,
    )


def output_kernel(
    chunk, hidden, down, mine, values, indices, spread, inverse_row, inverse_col,
    out, total, placed, wide, new,
):
    step = pl.program_id(0)
    replicas, strip, keep, _ = indices.shape
    half = strip * keep
    tall, breadth = new.shape
    spans = [slice(start, start + chunk) for start in range(0, breadth, chunk)]
    replica = lax.axis_index("replica")

    @pl.when(step == 0)
    def _():
        total[...] = jnp.zeros_like(total)

    place = lanes((half, chunk)).astype(jnp.float32)
    listed = [
        strip_offsets(indices, (replica + k) % replicas) for k in range(1, replicas)
    ]
    for n, span in enumerate(spans):
        even = odd = 0.0
        for k in range(replicas - 1):
            offset = dot(listed[k], spread[:, span])
            value = dot(values[k], spread[:, span])
            even = even + jnp.where(offset == place, value, 0.0)
            odd = odd + jnp.where(offset == place + TILE, value, 0.0)
        placed[n * tall : n * tall + half] = even.astype(jnp.bfloat16)
        placed[n * tall + half : (n + 1) * tall] = odd.astype(jnp.bfloat16)
    for n, span in enumerate(spans):
        wide[:, span] = dot(placed[n * tall : (n + 1) * tall], inverse_col[...]).astype(
            jnp.bfloat16
        )
    for span in spans:
        update = mine[:, span].astype(jnp.float32) + dot(inverse_row[...], wide[:, span])
        new[:, span] = (
            down[:, span].astype(jnp.float32) - (STEP_RATE / replicas) * update
        ).astype(jnp.bfloat16)
    for span in spans:
        total[:, span] += contract(hidden[...], new[:, span], 0)

    @pl.when(step == pl.num_programs(0) - 1)
    def _():
        size, rows, _ = out.shape
        for n in range(size):
            out[n] = total[n * rows : (n + 1) * rows].astype(out.dtype)


def output_pass(hidden, down, mine, values, indices, spread, mats, strip, chunk, size):
    rows, breadth = down.shape
    tall = strip * TILE
    replicas, _, keep, columns = indices.shape
    half = strip * keep
    count = hidden.shape[1]
    inverse_row, inverse_col = mats[3:]
    return pl.pallas_call(
        functools.partial(output_kernel, chunk),
        grid=(rows // tall,),
        out_shape=jax.ShapeDtypeStruct((size, count // size, breadth), jnp.bfloat16),
        in_specs=[
            pl.BlockSpec((tall, count), lambda i: (i, 0)),
            pl.BlockSpec((tall, breadth), lambda i: (i, 0)),
            pl.BlockSpec((tall, breadth), lambda i: (i, 0)),
            pl.BlockSpec((replicas - 1, half, columns), lambda i: (0, i, 0)),
            pl.BlockSpec((replicas, strip, keep, columns), lambda i: (0, i, 0, 0)),
            whole_block(spread),
            whole_block(inverse_row),
            whole_block(inverse_col),
        ],
        out_specs=pl.BlockSpec((size, count // size, breadth), lambda i: (0, 0, 0)),
        scratch_shapes=[
            pltpu.VMEM((count, breadth), jnp.float32),
            pltpu.VMEM((tall * (breadth // chunk), chunk), jnp.bfloat16),
            pltpu.VMEM((tall, breadth), jnp.bfloat16),
            pltpu.VMEM((tall, breadth), jnp.bfloat16),
        ],
        name="output_pass",
    )(hidden, down, mine, values, indices, spread, inverse_row, inverse_col)


def on_device(
    tokens, next_tokens, cotangent, gate_weight, up_weight, down_weight, momentum, indices
):
    size = lax.axis_size("tensor")
    replicas = lax.axis_size("replica")
    count, share = tokens.shape
    nexts = next_tokens.shape[0]
    breadth = share * size
    tile_rows, tile_cols, keep = indices.shape[1:]
    strip = next(n for n in (4, 2, 1) if tile_rows % n == 0)
    chunk = next(n for n in (256, 128) if breadth % n == 0)

    turned = next_tokens.T
    block = jnp.concatenate(
        [tokens.T, jnp.concatenate([turned[: share // 2], turned[share // 2 :]], axis=1)], axis=0
    )
    grads, hidden, next_hidden = hidden_pass(
        block, cotangent.T, gate_weight, up_weight, nexts, size
    )
    grads = grads.reshape(breadth, count)
    indices = jnp.swapaxes(indices, 2, 3)
    spread = jnp.asarray(np.kron(np.eye(tile_cols), np.ones((1, TILE))), jnp.bfloat16)
    mats = tables(strip, chunk)
    kept, mine, sent = moment_pass(
        hidden, grads, momentum, indices, spread, mats, strip, chunk
    )
    values = exchange(sent, replicas)
    partial = output_pass(
        next_hidden, down_weight, mine, values, indices, spread, mats, strip, chunk, size
    )
    output = scatter_sum(partial)
    return (output, kept)


def solution(mesh):
    return jax.shard_map(
        on_device,
        mesh=mesh,
        in_specs=(
            P("replica", "tensor"),
            P("replica", "tensor"),
            P("replica", "tensor"),
            P(None, "tensor"),
            P(None, "tensor"),
            P("tensor", None),
            P("replica", "tensor", None),
            P(None, "tensor", None, None),
        ),
        out_specs=(P(("replica", "tensor"), None), P("replica", "tensor", None)),
        check_vma=False,
    )
```

```python
import functools

import jax
import jax.numpy as jnp
import numpy as np
from jax import lax
from jax.experimental import pallas as pl
from jax.experimental.pallas import tpu as pltpu
from jax.sharding import PartitionSpec as P

TILE = 64
BETA_DECAY = 0.9
STEP_RATE = 0.1
MESH = pl.DeviceIdType.MESH
VMEM = pl.BlockSpec(memory_space=pltpu.VMEM)


def cosine_table():
    freq = np.arange(TILE)[:, None]
    place = np.arange(TILE)[None, :]
    table = np.cos(np.pi * (2.0 * place + 1.0) * freq / (2.0 * TILE))
    return table * np.where(freq == 0, np.sqrt(1.0 / TILE), np.sqrt(2.0 / TILE))


def split_bf16(table):
    high = jnp.asarray(table, jnp.float32).astype(jnp.bfloat16)
    rest = jnp.asarray(table, jnp.float32) - high.astype(jnp.float32)
    return high, rest.astype(jnp.bfloat16)


def tables(strip, chunk):
    table = cosine_table()
    across = np.kron(np.eye(chunk // TILE), table)
    down = np.concatenate(
        [np.kron(np.eye(strip), table[0::2]), np.kron(np.eye(strip), table[1::2])], axis=0
    )
    row_high, row_low = split_bf16(down)
    col_high, col_low = split_bf16(across.T)
    row = jnp.concatenate([row_high, row_low], axis=1)
    inverse_row = jnp.asarray(down.T, jnp.float32).astype(jnp.bfloat16)
    inverse_col = jnp.asarray(across, jnp.float32).astype(jnp.bfloat16)
    return row, col_high, col_low, inverse_row, inverse_col


def flip(index, bits):
    bit = 1
    while bit <= bits:
        if bits & bit:
            index = index + bit - 2 * bit * ((index // bit) % 2)
        bit *= 2
    return index


def greet(axis, others):
    barrier = pltpu.get_barrier_semaphore()
    for other in others:
        pl.semaphore_signal(barrier, inc=1, device_id={axis: other}, device_id_type=MESH)
    pl.semaphore_wait(barrier, len(others))


def hidden_kernel(
    size, feature_block, grad_block, gate_weight, up_weight, grads, hidden, next_hidden,
    held, features, turned, gate, upper, send, recv, local,
):
    me = lax.axis_index("tensor")
    depth = size // 4
    z, x, core = me // 4, (me // 2) % 2, me % 2
    blocks, kept = (feature_block, grad_block), (held, grads)

    def slot(zz, xx, cc):
        return (zz * 2 + xx) * 2 + cc

    loads = [
        pltpu.make_async_copy(source, target, local.at[n])
        for n, (source, target) in enumerate(
            [
                (feature_block, held.at[me]),
                (grad_block, grads.at[me]),
                (gate_weight, gate),
                (up_weight, upper),
            ]
        )
    ]
    for load in loads:
        load.start()
    others = [flip(z, k) for k in range(1, depth)]
    side, twin = slot(z, 1 - x, core), slot(z, x, 1 - core)
    greet("tensor", [slot(zz, x, core) for zz in others] + [side, twin])
    copies = []

    def push(kind, which, target, source=None):
        copy = pltpu.make_async_remote_copy(
            src_ref=kept[kind].at[which] if source is None else source,
            dst_ref=kept[kind].at[which],
            send_sem=send.at[len(copies)],
            recv_sem=recv.at[kind, which],
            device_id={"tensor": target},
            device_id_type=MESH,
        )
        copy.start()
        copies.append(copy)

    def arrive(kind, which):
        pltpu.make_async_remote_copy(
            src_ref=blocks[kind],
            dst_ref=kept[kind].at[which],
            send_sem=send.at[0],
            recv_sem=recv.at[kind, which],
            device_id={"tensor": twin},
            device_id_type=MESH,
        ).wait_recv()

    for kind in range(2):
        for target in [side] + [slot(zz, x, core) for zz in others] + [twin]:
            push(kind, me, target, blocks[kind])
    for kind in range(2):
        for zz in others:
            which = slot(zz, x, core)
            arrive(kind, which)
            push(kind, which, side)
            push(kind, which, twin)
    for kind in range(2):
        for zz in [z] + others:
            which = slot(zz, 1 - x, core)
            arrive(kind, which)
            push(kind, which, twin)
    for load in loads:
        load.wait()
    for zz in [z] + others:
        arrive(0, slot(zz, x, 1 - core))
        arrive(0, slot(zz, 1 - x, 1 - core))
    share, count = grads.shape[1:]
    nexts = next_hidden.shape[1]
    split = share // 2
    for n in range(size):
        base = n * share
        features[base : base + share, :count] = held[n, :share]
        features[base : base + split, count:] = held[n, share:, :nexts]
        features[base + split : base + share, count:] = held[n, share:, nexts:]
    turned[...] = features[...].T
    wide = dot(turned[...], gate[...])
    mixed = (wide / (1.0 + jnp.exp(-wide)) * dot(turned[...], upper[...])).astype(jnp.bfloat16).T
    hidden[...] = mixed[:, :count]
    next_hidden[...] = mixed[:, count:]
    for zz in [z] + others:
        arrive(1, slot(zz, x, 1 - core))
        arrive(1, slot(zz, 1 - x, 1 - core))
    for copy in copies:
        copy.wait_send()


def hidden_pass(feature_block, grad_block, gate_weight, up_weight, nexts, size):
    share, count = grad_block.shape
    breadth, width = gate_weight.shape
    kind = jnp.bfloat16
    hbm = pl.BlockSpec(memory_space=pl.ANY)
    return pl.pallas_call(
        functools.partial(hidden_kernel, size),
        out_shape=(
            jax.ShapeDtypeStruct((size, share, count), kind),
            jax.ShapeDtypeStruct((width, count), kind),
            jax.ShapeDtypeStruct((width, nexts), kind),
        ),
        in_specs=[VMEM, VMEM, hbm, hbm],
        out_specs=(VMEM, VMEM, VMEM),
        scratch_shapes=[
            pltpu.VMEM((size,) + feature_block.shape, kind),
            pltpu.VMEM((breadth, count + nexts), kind),
            pltpu.VMEM((count + nexts, breadth), kind),
            pltpu.VMEM(gate_weight.shape, kind),
            pltpu.VMEM(up_weight.shape, kind),
            pltpu.SemaphoreType.DMA((2 * size,)),
            pltpu.SemaphoreType.DMA((2, size)),
            pltpu.SemaphoreType.DMA((4,)),
        ],
        compiler_params=pltpu.CompilerParams(collective_id=0, has_side_effects=True),
        name="hidden_pass",
    )(feature_block, grad_block, gate_weight, up_weight)


def dot(a, b):
    return jnp.dot(a, b, preferred_element_type=jnp.float32)


def contract(a, b, dim):
    return lax.dot_general(
        a, b, (((dim,), (dim,)), ((), ())), preferred_element_type=jnp.float32
    )


def lanes(shape):
    return lax.broadcasted_iota(jnp.int32, shape, 1) % TILE


def strip_offsets(indices, which):
    strip, keep, columns = indices.shape[1:]
    first = lax.broadcasted_iota(jnp.int32, (keep, columns), 0) * (TILE * TILE // keep)
    listed = [
        (indices[which, n] - first).astype(jnp.float32).astype(jnp.bfloat16) for n in range(strip)
    ]
    return jnp.concatenate(listed, axis=0)


def moment_kernel(
    chunk, hidden, grads, momentum, indices, spread, gather, row, col_high, col_low,
    inverse_row, inverse_col, kept, mine, values_out,
    moment, mixed, offset, picked, stacked, pair, sent, received, send, recv,
):
    tall, breadth = moment.shape
    step = pl.program_id(0)
    replicas = indices.shape[0]
    steps = sent.shape[0]
    replica = lax.axis_index("replica")

    @pl.when(step == 0)
    def _():
        greet("replica", [(replica + k) % replicas for k in range(1, replicas)])

    half = tall // 2
    spans = [slice(start, start + chunk) for start in range(0, breadth, chunk)]
    own_offsets = strip_offsets(indices, lax.axis_index("replica"))
    for span in spans:
        offset[:, span] = dot(own_offsets, spread[:, span])
    for span in spans:
        moment[:, span] = BETA_DECAY * momentum[0, :, span].astype(jnp.float32) + contract(
            hidden[...], grads[span, :], 1
        )
    for k, span in enumerate(spans):
        rounded = moment[:, span].astype(jnp.bfloat16)
        mixed[k * tall : (k + 1) * tall] = dot(
            row[...], jnp.concatenate([rounded, rounded], axis=0)
        ).astype(jnp.bfloat16)
    place = lanes((half, chunk)).astype(jnp.float32)
    for k, span in enumerate(spans):
        part = mixed[k * tall : (k + 1) * tall]
        spectrum = dot(part, col_high[...]) + dot(part, col_low[...])
        where = offset[:, span]
        values = jnp.where(
            where == place,
            spectrum[:half],
            jnp.where(where == place + TILE, spectrum[half:], 0.0),
        ).astype(jnp.bfloat16)
        picked[:, span] = values
        stacked[k * half : (k + 1) * half] = values
    sent[step] = dot(picked[...], gather[...]).astype(jnp.bfloat16)
    for k, span in enumerate(spans):
        wide = dot(stacked[k * half : (k + 1) * half], inverse_col[...])
        odd = offset[:, span] >= TILE
        pair[:half, span] = jnp.where(odd, 0.0, wide).astype(jnp.bfloat16)
        pair[half:, span] = jnp.where(odd, wide, 0.0).astype(jnp.bfloat16)
    for span in spans:
        own = dot(inverse_row[...], pair[:, span])
        kept[0, :, span] = (moment[:, span] - own).astype(jnp.bfloat16)
        mine[:, span] = own.astype(jnp.bfloat16)

    def transfer(which, k):
        return pltpu.make_async_remote_copy(
            src_ref=sent.at[which],
            dst_ref=received.at[k - 1, which],
            send_sem=send.at[k - 1, which],
            recv_sem=recv.at[k - 1, which],
            device_id={"replica": (replica - k + replicas) % replicas},
            device_id_type=MESH,
        )

    for k in range(1, replicas):
        transfer(step, k).start()

    @pl.when(step == steps - 1)
    def _():
        for k in range(1, replicas):
            for which in range(steps):
                transfer(which, k).wait()
                values_out[k - 1, which] = received[k - 1, which]


def whole_block(array):
    return pl.BlockSpec(array.shape, lambda i: (0,) * array.ndim)


def moment_pass(hidden, grads, momentum, indices, spread, mats, strip, chunk):
    rows, breadth = momentum.shape[1:]
    tall = strip * TILE
    replicas, _, keep, columns = indices.shape
    half = strip * keep
    row, col_high, col_low, inverse_row, inverse_col = mats
    gather = spread.T
    return pl.pallas_call(
        functools.partial(moment_kernel, chunk),
        grid=(rows // tall,),
        out_shape=(
            jax.ShapeDtypeStruct((1, rows, breadth), jnp.bfloat16),
            jax.ShapeDtypeStruct((rows, breadth), jnp.bfloat16),
            jax.ShapeDtypeStruct((replicas - 1, rows // tall, half, columns), jnp.bfloat16),
        ),
        in_specs=[
            pl.BlockSpec((tall, hidden.shape[1]), lambda i: (i, 0)),
            whole_block(grads),
            pl.BlockSpec((1, tall, breadth), lambda i: (0, i, 0)),
            pl.BlockSpec((replicas, strip, keep, columns), lambda i: (0, i, 0, 0)),
            whole_block(spread),
            whole_block(gather),
            whole_block(row),
            whole_block(col_high),
            whole_block(col_low),
            whole_block(inverse_row),
            whole_block(inverse_col),
        ],
        out_specs=(
            pl.BlockSpec((1, tall, breadth), lambda i: (0, i, 0)),
            pl.BlockSpec((tall, breadth), lambda i: (i, 0)),
            pl.BlockSpec(
                (replicas - 1, rows // tall, half, columns), lambda i: (0, 0, 0, 0)
            ),
        ),
        scratch_shapes=[
            pltpu.VMEM((tall, breadth), jnp.float32),
            pltpu.VMEM((tall * (breadth // chunk), chunk), jnp.bfloat16),
            pltpu.VMEM((half, breadth), jnp.float32),
            pltpu.VMEM((half, breadth), jnp.bfloat16),
            pltpu.VMEM((half * (breadth // chunk), chunk), jnp.bfloat16),
            pltpu.VMEM((tall, breadth), jnp.bfloat16),
            pltpu.VMEM((rows // tall, half, columns), jnp.bfloat16),
            pltpu.VMEM((replicas - 1, rows // tall, half, columns), jnp.bfloat16),
            pltpu.SemaphoreType.DMA((replicas - 1, rows // tall)),
            pltpu.SemaphoreType.DMA((replicas - 1, rows // tall)),
        ],
        compiler_params=pltpu.CompilerParams(collective_id=1, has_side_effects=True),
        name="moment_pass",
    )(
        hidden, grads, momentum, indices, spread, gather, row, col_high, col_low, inverse_row,
        inverse_col,
    )


def output_kernel(
    chunk, size, hidden, down, mine, values, indices, spread, inverse_row, inverse_col,
    out, placed, wide, new, stage, held, send, recv,
):
    step = pl.program_id(0)
    steps = stage.shape[0]
    replicas = indices.shape[0]
    rows, breadth = new.shape
    tall = inverse_row.shape[0]
    half = tall // 2
    strips = rows // tall
    spans = [slice(start, start + chunk) for start in range(0, breadth, chunk)]
    replica = lax.axis_index("replica")
    me = lax.axis_index("tensor")
    barrier = pltpu.get_barrier_semaphore()

    @pl.when(step == 0)
    def _():
        for k in range(1, size):
            pl.semaphore_signal(
                barrier, inc=1, device_id={"tensor": (me + k) % size}, device_id_type=MESH
            )

    place = lanes((rows // 2, chunk)).astype(jnp.float32)
    listed = [strip_offsets(indices, (replica + k) % replicas) for k in range(1, replicas)]
    for n, span in enumerate(spans):
        even = odd = 0.0
        for k in range(replicas - 1):
            offset = dot(listed[k], spread[:, span])
            value = dot(values[k], spread[:, span])
            even = even + jnp.where(offset == place, value, 0.0)
            odd = odd + jnp.where(offset == place + TILE, value, 0.0)
        even, odd = even.astype(jnp.bfloat16), odd.astype(jnp.bfloat16)
        for m in range(strips):
            base = n * rows + m * tall
            placed[base : base + half] = even[m * half : (m + 1) * half]
            placed[base + half : base + tall] = odd[m * half : (m + 1) * half]
    for n, span in enumerate(spans):
        wide[:, span] = dot(placed[n * rows : (n + 1) * rows], inverse_col[...]).astype(
            jnp.bfloat16
        )
    for m in range(strips):
        band = slice(m * tall, (m + 1) * tall)
        update = mine[band].astype(jnp.float32) + dot(inverse_row[...], wide[band])
        new[band] = (
            down[band].astype(jnp.float32) - (STEP_RATE / replicas) * update
        ).astype(jnp.bfloat16)
    part = contract(hidden[...], new[...], 0).astype(jnp.bfloat16)
    short = out.shape[0]
    for n in range(size):
        stage[step, n] = part[n * short : (n + 1) * short]

    @pl.when(step == 0)
    def _():
        pl.semaphore_wait(barrier, size - 1)

    def transfer(which, k):
        target = (me + k) % size
        return pltpu.make_async_remote_copy(
            src_ref=stage.at[which, target],
            dst_ref=held.at[which, k - 1],
            send_sem=send.at[which, k - 1],
            recv_sem=recv.at[which, k - 1],
            device_id={"tensor": target},
            device_id_type=MESH,
        )

    for k in range(1, size):
        transfer(step, k).start()

    @pl.when(step == steps - 1)
    def _():
        for which in range(steps):
            total = stage[which, me].astype(jnp.float32)
            for k in range(1, size):
                transfer(which, k).wait()
                total = total + held[which, k - 1].astype(jnp.float32)
            out[:, which * breadth : (which + 1) * breadth] = total.astype(out.dtype)


def output_pass(hidden, down, mine, values, indices, spread, mats, chunk, size):
    rows, breadth = down.shape
    columns = spread.shape[0]
    part = 2 * chunk if breadth % (2 * chunk) == 0 else chunk
    steps = breadth // part
    short = hidden.shape[1] // size
    inverse_row, inverse_col = mats[3:]
    kind = jnp.bfloat16
    return pl.pallas_call(
        functools.partial(output_kernel, chunk, size),
        grid=(steps,),
        out_shape=jax.ShapeDtypeStruct((short, breadth), kind),
        in_specs=[
            whole_block(hidden),
            pl.BlockSpec((rows, part), lambda i: (0, i)),
            pl.BlockSpec((rows, part), lambda i: (0, i)),
            whole_block(values),
            whole_block(indices),
            pl.BlockSpec((columns, part), lambda i: (0, i)),
            whole_block(inverse_row),
            whole_block(inverse_col),
        ],
        out_specs=pl.BlockSpec((short, breadth), lambda i: (0, 0)),
        scratch_shapes=[
            pltpu.VMEM((rows * (part // chunk), chunk), kind),
            pltpu.VMEM((rows, part), kind),
            pltpu.VMEM((rows, part), kind),
            pltpu.VMEM((steps, size, short, part), kind),
            pltpu.VMEM((steps, size - 1, short, part), kind),
            pltpu.SemaphoreType.DMA((steps, size - 1)),
            pltpu.SemaphoreType.DMA((steps, size - 1)),
        ],
        compiler_params=pltpu.CompilerParams(collective_id=2, has_side_effects=True),
        name="output_pass",
    )(hidden, down, mine, values, indices, spread, inverse_row, inverse_col)


def on_device(
    tokens, next_tokens, cotangent, gate_weight, up_weight, down_weight, momentum, indices
):
    size = lax.axis_size("tensor")
    replicas = lax.axis_size("replica")
    count, share = tokens.shape
    nexts = next_tokens.shape[0]
    breadth = share * size
    tile_rows, tile_cols, keep = indices.shape[1:]
    strip = next(n for n in (4, 2, 1) if tile_rows % n == 0)
    chunk = next(n for n in (256, 128) if breadth % n == 0)

    turned = next_tokens.T
    block = jnp.concatenate(
        [tokens.T, jnp.concatenate([turned[: share // 2], turned[share // 2 :]], axis=1)], axis=0
    )
    grads, hidden, next_hidden = hidden_pass(
        block, cotangent.T, gate_weight, up_weight, nexts, size
    )
    grads = grads.reshape(breadth, count)
    indices = jnp.swapaxes(indices, 2, 3)
    spread = jnp.asarray(np.kron(np.eye(tile_cols), np.ones((1, TILE))), jnp.bfloat16)
    mats = tables(strip, chunk)
    kept, mine, values = moment_pass(
        hidden, grads, momentum, indices, spread, mats, strip, chunk
    )
    values = values.reshape(replicas - 1, tile_rows * keep, tile_cols)
    output = output_pass(
        next_hidden, down_weight, mine, values, indices, spread, mats, chunk, size
    )
    return (output, kept)


def solution(mesh):
    return jax.shard_map(
        on_device,
        mesh=mesh,
        in_specs=(
            P("replica", "tensor"),
            P("replica", "tensor"),
            P("replica", "tensor"),
            P(None, "tensor"),
            P(None, "tensor"),
            P("tensor", None),
            P("replica", "tensor", None),
            P(None, "tensor", None, None),
        ),
        out_specs=(P(("replica", "tensor"), None), P("replica", "tensor", None)),
        check_vma=False,
    )
```

```python
import functools

import jax
import jax.numpy as jnp
import numpy as np
from jax import lax
from jax.experimental import pallas as pl
from jax.experimental.pallas import tpu as pltpu
from jax.sharding import PartitionSpec as P

TILE = 64
BETA_DECAY = 0.9
STEP_RATE = 0.1
MESH = pl.DeviceIdType.MESH
VMEM = pl.BlockSpec(memory_space=pltpu.VMEM)


def cosine_table():
    freq = np.arange(TILE)[:, None]
    place = np.arange(TILE)[None, :]
    table = np.cos(np.pi * (2.0 * place + 1.0) * freq / (2.0 * TILE))
    return table * np.where(freq == 0, np.sqrt(1.0 / TILE), np.sqrt(2.0 / TILE))


def split_bf16(table):
    high = jnp.asarray(table, jnp.float32).astype(jnp.bfloat16)
    rest = jnp.asarray(table, jnp.float32) - high.astype(jnp.float32)
    return high, rest.astype(jnp.bfloat16)


def tables(strip, chunk):
    table = cosine_table()
    across = np.kron(np.eye(chunk // TILE), table)
    down = np.concatenate(
        [np.kron(np.eye(strip), table[0::2]), np.kron(np.eye(strip), table[1::2])], axis=0
    )
    row_high, row_low = split_bf16(down)
    col_high, col_low = split_bf16(across.T)
    row = jnp.concatenate([row_high, row_low], axis=1)
    inverse_row = jnp.asarray(down.T, jnp.float32).astype(jnp.bfloat16)
    inverse_col = jnp.asarray(across, jnp.float32).astype(jnp.bfloat16)
    return row, col_high, col_low, inverse_row, inverse_col


def flip(index, bits):
    bit = 1
    while bit <= bits:
        if bits & bit:
            index = index + bit - 2 * bit * ((index // bit) % 2)
        bit *= 2
    return index


def greet(axis, others):
    barrier = pltpu.get_barrier_semaphore()
    for other in others:
        pl.semaphore_signal(barrier, inc=1, device_id={axis: other}, device_id_type=MESH)
    pl.semaphore_wait(barrier, len(others))


def hidden_kernel(
    size, feature_block, grad_block, gate_weight, up_weight, grads, hidden, next_hidden,
    held, features, turned, gate, upper, send, recv, local,
):
    me = lax.axis_index("tensor")
    depth = size // 4
    z, x, core = me // 4, (me // 2) % 2, me % 2
    blocks, kept = (feature_block, grad_block), (held, grads)

    def slot(zz, xx, cc):
        return (zz * 2 + xx) * 2 + cc

    loads = [
        pltpu.make_async_copy(source, target, local.at[n])
        for n, (source, target) in enumerate(
            [
                (feature_block, held.at[me]),
                (grad_block, grads.at[me]),
                (gate_weight, gate),
                (up_weight, upper),
            ]
        )
    ]
    for load in loads:
        load.start()
    others = [flip(z, k) for k in range(1, depth)]
    side, twin = slot(z, 1 - x, core), slot(z, x, 1 - core)
    greet("tensor", [slot(zz, x, core) for zz in others] + [side, twin])
    copies = []

    def push(kind, which, target, source=None):
        copy = pltpu.make_async_remote_copy(
            src_ref=kept[kind].at[which] if source is None else source,
            dst_ref=kept[kind].at[which],
            send_sem=send.at[len(copies)],
            recv_sem=recv.at[kind, which],
            device_id={"tensor": target},
            device_id_type=MESH,
        )
        copy.start()
        copies.append(copy)

    def arrive(kind, which):
        pltpu.make_async_remote_copy(
            src_ref=blocks[kind],
            dst_ref=kept[kind].at[which],
            send_sem=send.at[0],
            recv_sem=recv.at[kind, which],
            device_id={"tensor": twin},
            device_id_type=MESH,
        ).wait_recv()

    for kind in range(2):
        for target in [side] + [slot(zz, x, core) for zz in others] + [twin]:
            push(kind, me, target, blocks[kind])
    for kind in range(2):
        for zz in others:
            which = slot(zz, x, core)
            arrive(kind, which)
            push(kind, which, side)
            push(kind, which, twin)
    for kind in range(2):
        for zz in [z] + others:
            which = slot(zz, 1 - x, core)
            arrive(kind, which)
            push(kind, which, twin)
    for load in loads:
        load.wait()
    for zz in [z] + others:
        arrive(0, slot(zz, x, 1 - core))
        arrive(0, slot(zz, 1 - x, 1 - core))
    share, count = grads.shape[1:]
    nexts = next_hidden.shape[1]
    split = share // 2
    for n in range(size):
        base = n * share
        features[base : base + share, :count] = held[n, :share]
        features[base : base + split, count:] = held[n, share:, :nexts]
        features[base + split : base + share, count:] = held[n, share:, nexts:]
    turned[...] = features[...].T
    wide = dot(turned[...], gate[...])
    mixed = (wide / (1.0 + jnp.exp(-wide)) * dot(turned[...], upper[...])).astype(jnp.bfloat16).T
    hidden[...] = mixed[:, :count]
    next_hidden[...] = mixed[:, count:]
    for zz in [z] + others:
        arrive(1, slot(zz, x, 1 - core))
        arrive(1, slot(zz, 1 - x, 1 - core))
    for copy in copies:
        copy.wait_send()


def hidden_pass(feature_block, grad_block, gate_weight, up_weight, nexts, size):
    share, count = grad_block.shape
    breadth, width = gate_weight.shape
    kind = jnp.bfloat16
    hbm = pl.BlockSpec(memory_space=pl.ANY)
    return pl.pallas_call(
        functools.partial(hidden_kernel, size),
        out_shape=(
            jax.ShapeDtypeStruct((size, share, count), kind),
            jax.ShapeDtypeStruct((width, count), kind),
            jax.ShapeDtypeStruct((width, nexts), kind),
        ),
        in_specs=[VMEM, VMEM, hbm, hbm],
        out_specs=(VMEM, VMEM, VMEM),
        scratch_shapes=[
            pltpu.VMEM((size,) + feature_block.shape, kind),
            pltpu.VMEM((breadth, count + nexts), kind),
            pltpu.VMEM((count + nexts, breadth), kind),
            pltpu.VMEM(gate_weight.shape, kind),
            pltpu.VMEM(up_weight.shape, kind),
            pltpu.SemaphoreType.DMA((2 * size,)),
            pltpu.SemaphoreType.DMA((2, size)),
            pltpu.SemaphoreType.DMA((4,)),
        ],
        compiler_params=pltpu.CompilerParams(collective_id=0, has_side_effects=True),
        name="hidden_pass",
    )(feature_block, grad_block, gate_weight, up_weight)


def dot(a, b):
    return jnp.dot(a, b, preferred_element_type=jnp.float32)


def contract(a, b, dim):
    return lax.dot_general(
        a, b, (((dim,), (dim,)), ((), ())), preferred_element_type=jnp.float32
    )


def lanes(shape):
    return lax.broadcasted_iota(jnp.int32, shape, 1) % TILE


def strip_offsets(indices, which):
    strip, keep, columns = indices.shape[1:]
    first = lax.broadcasted_iota(jnp.int32, (keep, columns), 0) * (TILE * TILE // keep)
    listed = [
        (indices[which, n] - first).astype(jnp.float32).astype(jnp.bfloat16) for n in range(strip)
    ]
    return jnp.concatenate(listed, axis=0)


def moment_kernel(
    chunk, hidden, grads, momentum, indices, spread, gather, row, col_high, col_low,
    inverse_row, inverse_col, kept, mine, sent,
    moment, mixed, offset, picked, stacked, pair,
):
    tall, breadth = moment.shape
    half = tall // 2
    spans = [slice(start, start + chunk) for start in range(0, breadth, chunk)]
    own_offsets = strip_offsets(indices, lax.axis_index("replica"))
    for span in spans:
        offset[:, span] = dot(own_offsets, spread[:, span])
    for span in spans:
        moment[:, span] = BETA_DECAY * momentum[0, :, span].astype(jnp.float32) + contract(
            hidden[...], grads[span, :], 1
        )
    for k, span in enumerate(spans):
        rounded = moment[:, span].astype(jnp.bfloat16)
        mixed[k * tall : (k + 1) * tall] = dot(
            row[...], jnp.concatenate([rounded, rounded], axis=0)
        ).astype(jnp.bfloat16)
    place = lanes((half, chunk)).astype(jnp.float32)
    for k, span in enumerate(spans):
        part = mixed[k * tall : (k + 1) * tall]
        spectrum = dot(part, col_high[...]) + dot(part, col_low[...])
        where = offset[:, span]
        values = jnp.where(
            where == place,
            spectrum[:half],
            jnp.where(where == place + TILE, spectrum[half:], 0.0),
        ).astype(jnp.bfloat16)
        picked[:, span] = values
        stacked[k * half : (k + 1) * half] = values
    sent[...] = dot(picked[...], gather[...]).astype(jnp.bfloat16)
    for k, span in enumerate(spans):
        wide = dot(stacked[k * half : (k + 1) * half], inverse_col[...])
        odd = offset[:, span] >= TILE
        pair[:half, span] = jnp.where(odd, 0.0, wide).astype(jnp.bfloat16)
        pair[half:, span] = jnp.where(odd, wide, 0.0).astype(jnp.bfloat16)
    for span in spans:
        own = dot(inverse_row[...], pair[:, span])
        kept[0, :, span] = (moment[:, span] - own).astype(jnp.bfloat16)
        mine[:, span] = own.astype(jnp.bfloat16)


def whole_block(array):
    return pl.BlockSpec(array.shape, lambda i: (0,) * array.ndim)


def moment_pass(hidden, grads, momentum, indices, spread, mats, strip, chunk):
    rows, breadth = momentum.shape[1:]
    tall = strip * TILE
    replicas, _, keep, columns = indices.shape
    half = strip * keep
    row, col_high, col_low, inverse_row, inverse_col = mats
    gather = spread.T
    return pl.pallas_call(
        functools.partial(moment_kernel, chunk),
        grid=(rows // tall,),
        out_shape=(
            jax.ShapeDtypeStruct((1, rows, breadth), jnp.bfloat16),
            jax.ShapeDtypeStruct((rows, breadth), jnp.bfloat16),
            jax.ShapeDtypeStruct((rows // 2, columns), jnp.bfloat16),
        ),
        in_specs=[
            pl.BlockSpec((tall, hidden.shape[1]), lambda i: (i, 0)),
            whole_block(grads),
            pl.BlockSpec((1, tall, breadth), lambda i: (0, i, 0)),
            pl.BlockSpec((replicas, strip, keep, columns), lambda i: (0, i, 0, 0)),
            whole_block(spread),
            whole_block(gather),
            whole_block(row),
            whole_block(col_high),
            whole_block(col_low),
            whole_block(inverse_row),
            whole_block(inverse_col),
        ],
        out_specs=(
            pl.BlockSpec((1, tall, breadth), lambda i: (0, i, 0)),
            pl.BlockSpec((tall, breadth), lambda i: (i, 0)),
            pl.BlockSpec((half, columns), lambda i: (i, 0)),
        ),
        scratch_shapes=[
            pltpu.VMEM((tall, breadth), jnp.float32),
            pltpu.VMEM((tall * (breadth // chunk), chunk), jnp.bfloat16),
            pltpu.VMEM((half, breadth), jnp.float32),
            pltpu.VMEM((half, breadth), jnp.bfloat16),
            pltpu.VMEM((half * (breadth // chunk), chunk), jnp.bfloat16),
            pltpu.VMEM((tall, breadth), jnp.bfloat16),
        ],
        name="moment_pass",
    )(
        hidden, grads, momentum, indices, spread, gather, row, col_high, col_low, inverse_row,
        inverse_col,
    )


def output_kernel(
    chunk, size, hidden, down, mine, values, indices, spread, inverse_row, inverse_col,
    out, placed, wide, new, stage, held, send, recv, offset, received, pass_send, pass_recv,
):
    step = pl.program_id(0)
    steps = stage.shape[0]
    replicas = indices.shape[0]
    rows, breadth = new.shape
    tall = inverse_row.shape[0]
    half = tall // 2
    strips = rows // tall
    spans = [slice(start, start + chunk) for start in range(0, breadth, chunk)]
    replica = lax.axis_index("replica")
    me = lax.axis_index("tensor")
    barrier = pltpu.get_barrier_semaphore()

    def share(k):
        return pltpu.make_async_remote_copy(
            src_ref=values,
            dst_ref=received.at[k - 1],
            send_sem=pass_send.at[k - 1],
            recv_sem=pass_recv.at[k - 1],
            device_id={"replica": (replica - k + replicas) % replicas},
            device_id_type=MESH,
        )

    @pl.when(step == 0)
    def _():
        for k in range(1, size):
            pl.semaphore_signal(
                barrier, inc=1, device_id={"tensor": (me + k) % size}, device_id_type=MESH
            )
        for k in range(1, replicas):
            pl.semaphore_signal(
                barrier, inc=1, device_id={"replica": (replica + k) % replicas},
                device_id_type=MESH,
            )
        pl.semaphore_wait(barrier, size + replicas - 2)
        for k in range(1, replicas):
            share(k).start()

    place = lanes((rows // 2, chunk)).astype(jnp.float32)
    listed = [strip_offsets(indices, (replica + k) % replicas) for k in range(1, replicas)]
    for k in range(replicas - 1):
        offset[k] = dot(listed[k], spread[...])

    @pl.when(step == 0)
    def _():
        for k in range(1, replicas):
            share(k).wait()

    for n, span in enumerate(spans):
        even = odd = 0.0
        for k in range(replicas - 1):
            where = offset[k, :, span]
            value = dot(received[k], spread[:, span])
            even = even + jnp.where(where == place, value, 0.0)
            odd = odd + jnp.where(where == place + TILE, value, 0.0)
        even, odd = even.astype(jnp.bfloat16), odd.astype(jnp.bfloat16)
        for m in range(strips):
            base = n * rows + m * tall
            placed[base : base + half] = even[m * half : (m + 1) * half]
            placed[base + half : base + tall] = odd[m * half : (m + 1) * half]
    for n, span in enumerate(spans):
        wide[:, span] = dot(placed[n * rows : (n + 1) * rows], inverse_col[...]).astype(
            jnp.bfloat16
        )
    for m in range(strips):
        band = slice(m * tall, (m + 1) * tall)
        update = mine[band].astype(jnp.float32) + dot(inverse_row[...], wide[band])
        new[band] = (
            down[band].astype(jnp.float32) - (STEP_RATE / replicas) * update
        ).astype(jnp.bfloat16)
    part = contract(hidden[...], new[...], 0).astype(jnp.bfloat16)
    short = out.shape[0]
    for n in range(size):
        stage[step, n] = part[n * short : (n + 1) * short]

    def transfer(which, k):
        target = (me + k) % size
        return pltpu.make_async_remote_copy(
            src_ref=stage.at[which, target],
            dst_ref=held.at[which, k - 1],
            send_sem=send.at[which, k - 1],
            recv_sem=recv.at[which, k - 1],
            device_id={"tensor": target},
            device_id_type=MESH,
        )

    for k in range(1, size):
        transfer(step, k).start()

    @pl.when(step == steps - 1)
    def _():
        for which in range(steps):
            total = stage[which, me].astype(jnp.float32)
            for k in range(1, size):
                transfer(which, k).wait()
                total = total + held[which, k - 1].astype(jnp.float32)
            out[:, which * breadth : (which + 1) * breadth] = total.astype(out.dtype)


def output_pass(hidden, down, mine, values, indices, spread, mats, chunk, size):
    rows, breadth = down.shape
    columns = spread.shape[0]
    part = 2 * chunk if breadth % (2 * chunk) == 0 else chunk
    steps = breadth // part
    short = hidden.shape[1] // size
    inverse_row, inverse_col = mats[3:]
    kind = jnp.bfloat16
    return pl.pallas_call(
        functools.partial(output_kernel, chunk, size),
        grid=(steps,),
        out_shape=jax.ShapeDtypeStruct((short, breadth), kind),
        in_specs=[
            whole_block(hidden),
            pl.BlockSpec((rows, part), lambda i: (0, i)),
            pl.BlockSpec((rows, part), lambda i: (0, i)),
            whole_block(values),
            whole_block(indices),
            pl.BlockSpec((columns, part), lambda i: (0, i)),
            whole_block(inverse_row),
            whole_block(inverse_col),
        ],
        out_specs=pl.BlockSpec((short, breadth), lambda i: (0, 0)),
        scratch_shapes=[
            pltpu.VMEM((rows * (part // chunk), chunk), kind),
            pltpu.VMEM((rows, part), kind),
            pltpu.VMEM((rows, part), kind),
            pltpu.VMEM((steps, size, short, part), kind),
            pltpu.VMEM((steps, size - 1, short, part), kind),
            pltpu.SemaphoreType.DMA((steps, size - 1)),
            pltpu.SemaphoreType.DMA((steps, size - 1)),
            pltpu.VMEM((indices.shape[0] - 1, rows // 2, part), jnp.float32),
            pltpu.VMEM((indices.shape[0] - 1,) + values.shape, kind),
            pltpu.SemaphoreType.DMA((indices.shape[0] - 1,)),
            pltpu.SemaphoreType.DMA((indices.shape[0] - 1,)),
        ],
        compiler_params=pltpu.CompilerParams(collective_id=2, has_side_effects=True),
        name="output_pass",
    )(hidden, down, mine, values, indices, spread, inverse_row, inverse_col)


def on_device(
    tokens, next_tokens, cotangent, gate_weight, up_weight, down_weight, momentum, indices
):
    size = lax.axis_size("tensor")
    replicas = lax.axis_size("replica")
    count, share = tokens.shape
    nexts = next_tokens.shape[0]
    breadth = share * size
    tile_rows, tile_cols, keep = indices.shape[1:]
    strip = next(n for n in (4, 2, 1) if tile_rows % n == 0)
    chunk = next(n for n in (256, 128) if breadth % n == 0)

    turned = next_tokens.T
    block = jnp.concatenate(
        [tokens.T, jnp.concatenate([turned[: share // 2], turned[share // 2 :]], axis=1)], axis=0
    )
    grads, hidden, next_hidden = hidden_pass(
        block, cotangent.T, gate_weight, up_weight, nexts, size
    )
    grads = grads.reshape(breadth, count)
    indices = jnp.swapaxes(indices, 2, 3)
    spread = jnp.asarray(np.kron(np.eye(tile_cols), np.ones((1, TILE))), jnp.bfloat16)
    mats = tables(strip, chunk)
    kept, mine, values = moment_pass(
        hidden, grads, momentum, indices, spread, mats, strip, chunk
    )
    output = output_pass(
        next_hidden, down_weight, mine, values, indices, spread, mats, chunk, size
    )
    return (output, kept)


def solution(mesh):
    return jax.shard_map(
        on_device,
        mesh=mesh,
        in_specs=(
            P("replica", "tensor"),
            P("replica", "tensor"),
            P("replica", "tensor"),
            P(None, "tensor"),
            P(None, "tensor"),
            P("tensor", None),
            P("replica", "tensor", None),
            P(None, "tensor", None, None),
        ),
        out_specs=(P(("replica", "tensor"), None), P("replica", "tensor", None)),
        check_vma=False,
    )
```
